32 devices in a mesh: gz: 2 (over core), gx: 4 (over z), gy: 4 (over y, x).
Axes of the slice: x: 2, y: 2, z: 4, core: 2. Of those that a mesh axis runs over, the one named last changes fastest.
Arguments:
- pair_repr: bfloat16 [8, 384, 384, 128], P('gz', 'gx', 'gy'), may hold values from -9 to 9
- seq_lengths: int32 [8], replicated, may hold values from 96 to 384
- weight_in: bfloat16 [128, 640], replicated, may hold values from -0.5 to 0.5
- weight_out: bfloat16 [128, 128], replicated, may hold values from -0.5 to 0.5
Outputs:
- updated: bfloat16 [8, 384, 384, 128], P('gz', 'gx', 'gy')
- magnitude: float32 [], replicated
The draws below stay inside these ranges and needn't reach their ends.
All inputs are finite; a program needn't handle non-finite values.
Results may differ from the reference program's by a relative error of at most 0.0034.
Values may be sent and summed in bfloat16 or wider, within the bound.
A program may use at most 384 MiB of HBM per device.

```python
import math
import jax
import jax.numpy as jnp
from jax import lax

C = 128
CH = 128
N = 384
BATCH = 8


def draw_pair_repr(key, part):
    split_keys = jax.random.split(jax.random.fold_in(key, 17), 3)
    row_ramp = 0.5 + jnp.arange(N, dtype=jnp.float32) / N
    row_scale = jnp.exp(jax.random.uniform(split_keys[1], (BATCH, N, 1, 1), jnp.float32, math.log(0.7), math.log(1.4)))
    col_scale = jnp.exp(jax.random.uniform(split_keys[2], (BATCH, 1, N, 1), jnp.float32, math.log(0.7), math.log(1.4)))
    base_values = jnp.clip(jax.random.normal(split_keys[0], (BATCH, N, N, C), jnp.float32), -3.0, 3.0)
    values = base_values * row_ramp[None, :, None, None] * row_scale * col_scale
    return values.astype(jnp.bfloat16)


def with_ends(array, key, least, top_value):
    longest = array.shape.index(max(array.shape))
    spots = []
    for shift in (0, 1):
        where = [jax.random.randint(jax.random.fold_in(key, axis), (), 0, length) for axis, length in enumerate(array.shape)]
        where[longest] = (where[longest] + shift) % array.shape[longest]
        spots.append(tuple(where))
    return array.at[spots[0]].set(least).at[spots[1]].set(top_value)


def noise(rng, extent, scale, most, held_as=jnp.bfloat16):
    array = scale * jax.random.normal(rng, extent, jnp.float32)
    return jnp.clip(array, min=-most, max=most).astype(held_as)


def setup_inputs(seed: int = 0) -> dict:
    seeds = jax.random.split(jax.random.key(seed), 5)
    pair_repr = draw_pair_repr(jax.random.fold_in(seeds[4], 71), 0)
    seq_lengths = with_ends(jax.random.randint(seeds[1], (BATCH,), N // 4, N + 1), jax.random.fold_in(seeds[1], 1), N // 4, N).astype(jnp.int32)
    weight_in = noise(seeds[2], (C, 4 * CH + C), C ** -0.5, 0.5)
    weight_out = noise(seeds[3], (CH, C), CH ** -0.5, 0.5)
    return dict(pair_repr=pair_repr, seq_lengths=seq_lengths, weight_in=weight_in, weight_out=weight_out)


def layer_norm(values):
    mean_value = lax.optimization_barrier(jnp.mean(values, axis=-1, keepdims=True))
    centered = values - mean_value
    variance = lax.optimization_barrier(jnp.mean(centered * centered, axis=-1, keepdims=True))
    return centered * lax.rsqrt(variance + 1e-05)

def reference(pair_repr, seq_lengths, weight_in, weight_out):

    def one_tensor(inputs):
        pair_one, length_one = inputs
        positions = jnp.arange(N, dtype=jnp.int32)
        row_live = (positions < length_one).astype(jnp.float32)
        pair_mask = (row_live[:, None] * row_live[None, :])[:, :, None]
        normed = layer_norm(pair_one.astype(jnp.float32)).astype(jnp.bfloat16)
        proj = jnp.dot(normed.reshape(N * N, C), weight_in, preferred_element_type=jnp.float32).reshape(N, N, 4 * CH + C)
        left_proj = (pair_mask * jax.nn.sigmoid(proj[..., CH:2 * CH]) * proj[..., :CH]).astype(jnp.bfloat16)
        right_proj = (pair_mask * jax.nn.sigmoid(proj[..., 3 * CH:4 * CH]) * proj[..., 2 * CH:3 * CH]).astype(jnp.bfloat16)
        gate_values = jax.nn.sigmoid(proj[..., 4 * CH:])
        triangle = jnp.einsum('kic,kjc->ijc', left_proj.astype(jnp.float32), right_proj.astype(jnp.float32), precision=lax.Precision.HIGHEST)
        tri_normed = layer_norm(triangle).astype(jnp.bfloat16)
        projected = jnp.dot(tri_normed.reshape(N * N, CH), weight_out, preferred_element_type=jnp.float32).reshape(N, N, C)
        update = pair_mask * gate_values * projected
        return (pair_one.astype(jnp.float32) + update).astype(jnp.bfloat16)
    updated = lax.map(one_tensor, (pair_repr, seq_lengths))
    entry_count = float(BATCH * N * N * C)
    magnitude = jnp.sum(jnp.abs(updated.astype(jnp.float32))) / entry_count
    return (updated, magnitude)
```

```python
import jax
import jax.numpy as jnp
from jax import lax
from jax.sharding import PartitionSpec as P


def layer_norm(values):
    mean_value = jnp.mean(values, axis=-1, keepdims=True)
    centered = values - mean_value
    variance = jnp.mean(centered * centered, axis=-1, keepdims=True)
    return centered * lax.rsqrt(variance + 1e-05)


def per_device(pair_repr, seq_lengths, weight_in, weight_out):
    batch_dev, row_count, col_count, channels = pair_repr.shape
    hidden = weight_out.shape[0]
    row_first = lax.axis_index("gx") * row_count
    col_first = lax.axis_index("gy") * col_count
    my_lengths = lax.dynamic_slice_in_dim(seq_lengths, lax.axis_index("gz") * batch_dev, batch_dev)
    row_at = row_first + jnp.arange(row_count, dtype=jnp.int32)
    col_at = col_first + jnp.arange(col_count, dtype=jnp.int32)

    def gated(normed, first, mask):
        part = weight_in[:, first : first + 2 * hidden]
        proj = jnp.einsum("ijc,cd->ijd", normed, part, preferred_element_type=jnp.float32)
        return (mask * jax.nn.sigmoid(proj[..., hidden:]) * proj[..., :hidden]).astype(
            jnp.bfloat16
        )

    masks, normed, gathered, shares = [], [], [], []
    for b in range(batch_dev):
        row_live = (row_at < my_lengths[b]).astype(jnp.float32)
        col_live = (col_at < my_lengths[b]).astype(jnp.float32)
        masks.append(row_live[:, None, None] * col_live[None, :, None])
        normed.append(layer_norm(pair_repr[b].astype(jnp.float32)).astype(jnp.bfloat16))
        left = gated(normed[b], 0, masks[b])
        gathered.append(lax.all_gather(left, "gy", axis=1, tiled=True))
    for b in range(batch_dev):
        right = gated(normed[b], 2 * hidden, masks[b])
        partial = jnp.einsum(
            "kic,kjc->ijc", gathered[b], right, preferred_element_type=jnp.float32
        ).astype(jnp.bfloat16)
        shares.append(lax.psum_scatter(partial, "gx", scatter_dimension=0, tiled=True))
    outs, total = [], jnp.float32(0)
    for b in range(batch_dev):
        gate_values = jax.nn.sigmoid(
            jnp.einsum(
                "ijc,cd->ijd", normed[b], weight_in[:, 4 * hidden :],
                preferred_element_type=jnp.float32,
            )
        )
        tri_normed = layer_norm(shares[b].astype(jnp.float32)).astype(jnp.bfloat16)
        projected = jnp.einsum(
            "ijc,cd->ijd", tri_normed, weight_out, preferred_element_type=jnp.float32
        )
        update = masks[b] * gate_values * projected
        one = (pair_repr[b].astype(jnp.float32) + update).astype(jnp.bfloat16)
        outs.append(one)
        total = total + jnp.sum(jnp.abs(one.astype(jnp.float32)))
    updated = jnp.stack(outs)
    mag_total = lax.psum(total, ("gz", "gx", "gy"))
    entry_count = (
        batch_dev
        * lax.axis_size("gz")
        * row_count
        * lax.axis_size("gx")
        * col_count
        * lax.axis_size("gy")
        * channels
    )
    magnitude = mag_total / float(entry_count)
    return (updated, magnitude)


def solution(mesh):
    return jax.shard_map(
        per_device,
        mesh=mesh,
        in_specs=(P("gz", "gx", "gy", None), P(), P(), P()),
        out_specs=(P("gz", "gx", "gy", None), P()),
        check_vma=False,
    )
```
